128 devices in a mesh: rows: 16 (over y, z_lo, core), reg: 8 (over z_hi, x).
Axes of the slice: x: 4, y: 4, z: 4 (z_hi: 2, z_lo: 2; z = z_hi * 2 + z_lo), core: 2. Of those that a mesh axis runs over, the one named last changes fastest.
Arguments:
- snapshots: bfloat16 [131072, 2048], P('rows', 'reg'), may hold values from -6 to 6
- rates: bfloat16 [131072, 2048], P('rows', 'reg'), may hold values from -6 to 6
- basis: bfloat16 [131072, 128], P('rows'), may hold values from -0.015625 to 0.015625
Outputs:
- gram: float32 [8384, 8384], P('rows', 'reg')
- rhs: float32 [8384, 128], P('rows')
The draws below stay inside these ranges and needn't reach their ends.
All inputs are finite; a program needn't handle non-finite values.
Results may differ from the reference program's by a relative error of at most 0.0042.
Values may be sent and summed in bfloat16 or wider, within the bound.
A program may use at most 64 MiB of HBM per device.

```python
import jax
import jax.numpy as jnp
import numpy as np

R = 128
NROWS = 131072
NT = 2048


def level_of(own_key, shape, pieces, low, high):
    level = 1.0
    for axis_at, blocks in pieces:
        steps = jax.random.uniform(jax.random.fold_in(jax.random.fold_in(own_key, 6), axis_at), (blocks,), jnp.float32, low / len(pieces), high / len(pieces))
        level = level * jnp.repeat(jnp.exp(steps), shape[axis_at] // blocks).reshape((-1,) + (1,) * (len(shape) - 1 - axis_at))
    return level


def bell_draw(own_key, extent, scale, most, cuts=(), dtype=jnp.bfloat16):
    level = level_of(own_key, extent, cuts, -0.22, 0.18) if cuts else 1.0
    drawn = jax.random.normal(own_key, extent, jnp.float32) * scale * level
    return jnp.minimum(jnp.maximum(drawn, -most), most).astype(dtype)


def setup_inputs(seed: int = 0) -> dict:
    key_of = jax.random.split(jax.random.key(seed), 4)
    snapshots = bell_draw(key_of[0], (NROWS, NT), 1.0, 6.0, ((0, 16), (1, 8)))
    rates = bell_draw(key_of[1], (NROWS, NT), 1.0, 6.0, ((0, 16), (1, 8)))
    basis = bell_draw(key_of[2], (NROWS, R), NROWS ** -0.5, 0.015625, ((0, 16),))
    return dict(snapshots=snapshots, rates=rates, basis=basis)


def make_features(states):
    upper_i, upper_j = np.triu_indices(states.shape[0])
    quad = jnp.take(states, upper_i, axis=0) * jnp.take(states, upper_j, axis=0)
    return jnp.concatenate([states, quad], axis=0).astype(jnp.bfloat16)


def reference(snapshots, rates, basis):
    states = jnp.dot(basis.T, snapshots, preferred_element_type=jnp.float32)
    moments = jnp.dot(basis.T, rates, preferred_element_type=jnp.float32).astype(jnp.bfloat16)
    features = make_features(states)
    gram = jnp.dot(features, features.T, preferred_element_type=jnp.float32) / float(NT)
    rhs = jnp.dot(features, moments.T, preferred_element_type=jnp.float32) / float(NT)
    return gram, rhs
```

```python
import jax
import jax.numpy as jnp
from jax import lax
from jax.experimental import pallas as pl
from jax.experimental.pallas import tpu as pltpu
from jax.sharding import PartitionSpec as P

MESH = pl.DeviceIdType.MESH
F32 = jnp.float32
BF16 = jnp.bfloat16
CHUNKS = 8


def device_at(x, y, z, c):
    return ((y * 2 + lax.rem(z, 2)) * 2 + c, lax.div(z, 2) * 4 + x)


def exchange_kernel(
    snap_hbm, rates_hbm, basis_hbm, states_out, moments_out,
    snap, rates, basis, basis_t, part_s, part_m, land_s, land_m,
    load_sem, send_s, recv_s, send_m, recv_m,
    sg_send, sg_recv, mg_send, mg_recv,
):
    rows, reg = lax.axis_index("rows"), lax.axis_index("reg")
    c = lax.rem(rows, 2)
    zl = lax.rem(lax.div(rows, 2), 2)
    y = lax.div(rows, 4)
    x = lax.rem(reg, 4)
    zh = lax.div(reg, 4)
    z = zh * 2 + zl

    def turn(v, d):
        return lax.rem(v + d, 4)

    group = [(dy, dz, dc) for dy in range(4) for dz in range(2) for dc in range(2)][1:]

    def group_row(dy, dz, dc):
        return (turn(y, dy) * 2 + lax.rem(zl + dz, 2)) * 2 + lax.rem(c + dc, 2)

    barrier = pltpu.get_barrier_semaphore()
    for dy, dz, dc in group:
        pl.semaphore_signal(barrier, inc=1, device_id=(group_row(dy, dz, dc), reg), device_id_type=MESH)
    for d in (1, 2, 3):
        pl.semaphore_signal(barrier, inc=1, device_id=device_at(turn(x, d), y, z, c), device_id_type=MESH)
    for d in (2, 3 + 2 * zl):
        pl.semaphore_signal(barrier, inc=1, device_id=device_at(x, y, turn(z, d), c), device_id_type=MESH)

    depth = snap_hbm.shape[0] // CHUNKS
    loads = {}
    for k in range(CHUNKS):
        at = pl.ds(k * depth, depth)
        for i, (src, dst) in enumerate(((basis_hbm, basis), (snap_hbm, snap))):
            loads[i, k] = pltpu.make_async_copy(src.at[at, :], dst.at[at, :], load_sem.at[i, k])
            loads[i, k].start()
    for k in range(CHUNKS):
        at = pl.ds(k * depth, depth)
        loads[2, k] = pltpu.make_async_copy(rates_hbm.at[at, :], rates.at[at, :], load_sem.at[2, k])
        loads[2, k].start()

    total = jnp.zeros((128, 256), F32)
    for k in range(CHUNKS):
        at = pl.ds(k * depth, depth)
        loads[0, k].wait()
        loads[1, k].wait()
        turned = basis[at, :].T
        basis_t[:, at] = turned
        total += jnp.dot(turned, snap[at, :], preferred_element_type=F32)
    part_s[...] = total.reshape(16, 8, 256)

    pl.semaphore_wait(barrier, 20)
    out_s = []
    for n, (dy, dz, dc) in enumerate(group):
        to = group_row(dy, dz, dc)
        copy = pltpu.make_async_remote_copy(
            src_ref=part_s.at[to], dst_ref=land_s.at[n], send_sem=send_s.at[n], recv_sem=recv_s.at[n],
            device_id=(to, reg), device_id_type=MESH,
        )
        copy.start()
        out_s.append(copy)

    total = jnp.zeros((128, 256), F32)
    for k in range(CHUNKS):
        at = pl.ds(k * depth, depth)
        loads[2, k].wait()
        total += jnp.dot(basis_t[:, at], rates[at, :], preferred_element_type=F32)
    for b in range(8):
        for h in range(2):
            part_m[b * 2 + h] = total[b * 16:(b + 1) * 16, h * 128:(h + 1) * 128]
    out_m = []
    for n, (dy, dz, dc) in enumerate(group):
        to = group_row(dy, dz, dc)
        copy = pltpu.make_async_remote_copy(
            src_ref=part_m.at[to], dst_ref=land_m.at[n], send_sem=send_m.at[n], recv_sem=recv_m.at[n],
            device_id=(to, reg), device_id_type=MESH,
        )
        copy.start()
        out_m.append(copy)

    first = (1 - c) * y + c * z
    second = (1 - c) * z + c * x
    third = (1 - c) * x + c * y

    def peer(stage, d):
        step0, step1 = (1 - c) * d, c * d
        if stage == 1:
            return device_at(x, turn(y, step0), turn(z, step1), c)
        if stage == 2:
            return device_at(turn(x, step1), y, turn(z, step0), c)
        return device_at(turn(x, step0), turn(y, step1), z, c)

    own = (third * 4 + second) * 4 + first
    pending = []

    def gather(buf, send, recv):
        def push(at, device, n):
            copy = pltpu.make_async_remote_copy(
                src_ref=buf.at[c, at], dst_ref=buf.at[c, at], send_sem=send.at[n], recv_sem=recv.at[n],
                device_id=device, device_id_type=MESH,
            )
            copy.start()
            pending.append(copy)

        def arrive(at, n):
            pltpu.make_async_remote_copy(
                src_ref=buf.at[c, at], dst_ref=buf.at[c, at], send_sem=send.at[n], recv_sem=recv.at[n],
                device_id=device_at(x, y, z, 1 - c), device_id_type=MESH,
            ).wait_recv()

        def arrive_twin(at, n):
            pltpu.make_async_remote_copy(
                src_ref=buf.at[1 - c, at], dst_ref=buf.at[1 - c, at], send_sem=send.at[n], recv_sem=recv.at[n],
                device_id=device_at(x, y, z, 1 - c), device_id_type=MESH,
            ).wait_recv()

        twin = device_at(x, y, z, 1 - c)

        def quad(a3, a2):
            return pl.ds((a3 * 4 + a2) * 4, 4)

        def stage1():
            for d in (1, 2, 3):
                push(pl.ds(own, 1), peer(1, d), d - 1)

        def stage2():
            for d in (1, 2, 3):
                arrive(pl.ds((third * 4 + second) * 4 + turn(first, 4 - d), 1), d - 1)
            mine = quad(third, second)
            for d in (1, 2, 3):
                push(mine, peer(2, d), 2 + d)
            for d in (1, 2, 3):
                push(mine, peer(3, d), 6 + (d - 1) * 4)
            push(mine, twin, 18)

        def stage3():
            for e in (1, 2, 3):
                at = quad(third, turn(second, 4 - e))
                arrive(at, 2 + e)
                for d in (1, 2, 3):
                    push(at, peer(3, d), 6 + (d - 1) * 4 + e)
                push(at, twin, 18 + e)

        def stage4():
            for e in range(4):
                for d in (1, 2, 3):
                    at = quad(turn(third, 4 - d), turn(second, 4 - e))
                    arrive(at, 6 + (d - 1) * 4 + e)
                    push(at, twin, 18 + d * 4 + e)

        t_second = c * z + (1 - c) * x
        t_third = c * x + (1 - c) * y

        def stage5():
            for d in range(4):
                for e in range(4):
                    at = quad(turn(t_third, 4 - d), turn(t_second, 4 - e))
                    arrive_twin(at, 18 + d * 4 + e)

        return stage1, stage2, stage3, stage4, stage5

    s_stages = gather(states_out, sg_send, sg_recv)
    m_stages = gather(moments_out, mg_send, mg_recv)

    piece = part_s[rows]
    for n in range(15):
        out_s[n].wait_recv()
    for n in range(15):
        piece += land_s[n]
    states_out[c, own] = piece
    s_stages[0]()
    piece = part_m[rows]
    for n in range(15):
        out_m[n].wait_recv()
    for n in range(15):
        piece += land_m[n]
    moments_out[c, own] = piece.astype(BF16)
    m_stages[0]()
    for s, m in zip(s_stages[1:], m_stages[1:]):
        s()
        m()
    for copy in out_s + out_m + pending:
        copy.wait_send()


def gram_kernel(states_ref, moments_ref, gram_ref, rhs_ref, split, rates, row_feat):
    step = pl.program_id(0)
    rank, times = 128, split.shape[1]
    height, width = row_feat.shape[0], gram_ref.shape[1]

    def one_hot(base, count):
        k = lax.broadcasted_iota(jnp.int32, (count, rank), 0) + base
        t = lax.broadcasted_iota(jnp.int32, (count, rank), 1)
        start = rank + t * rank - lax.div(t * (t - 1), 2)
        quad_i = (k >= start) & (k < start + rank - t)
        offset = jnp.sum(jnp.where(quad_i, (t - start).astype(F32), 0.0), axis=1, keepdims=True)
        j = k + offset.astype(jnp.int32)
        linear = k < rank
        pick_i = jnp.where(quad_i | (linear & (t == k)), 1.0, 0.0).astype(BF16)
        pick_j = jnp.where((t == j) & (k >= rank), 1.0, 0.0).astype(BF16)
        plus = jnp.where(linear[:, :1], 1.0, 0.0)
        return jnp.concatenate([pick_i, pick_i], axis=1), jnp.concatenate([pick_j, pick_j], axis=1), plus

    def build(base, count):
        pick_i, pick_j, plus = one_hot(base, count)
        for n in range(times // 256):
            w = split[:, n * 256:(n + 1) * 256]
            a = jnp.dot(pick_i, w, preferred_element_type=F32)
            b = jnp.dot(pick_j, w, preferred_element_type=F32) + plus
            yield n, (a * b).astype(BF16)

    @pl.when(step == 0)
    def _():
        for g in range(8):
            gx, gz = g % 4, g // 4
            for b in range(8):
                y, z = b // 2, gz * 2 + b % 2
                at0 = (gx * 4 + z) * 4 + y
                at1 = (y * 4 + gx) * 4 + z
                s = jnp.concatenate([states_ref[0, at0], states_ref[1, at1]], axis=0)
                hi = s.astype(BF16)
                lo = (s - hi.astype(F32)).astype(BF16)
                cols = slice(g * 256, (g + 1) * 256)
                split[b * 16:(b + 1) * 16, cols] = hi
                split[rank + b * 16:rank + (b + 1) * 16, cols] = lo
                rates[b * 16:(b + 1) * 16, g * 256:g * 256 + 128] = moments_ref[0, at0]
                rates[b * 16:(b + 1) * 16, g * 256 + 128:(g + 1) * 256] = moments_ref[1, at1]
        for n, f in build(lax.axis_index("rows") * rhs_ref.shape[0], height):
            row_feat[:, n * 256:(n + 1) * 256] = f
        rhs = lax.dot_general(row_feat[...], rates[...], (((1,), (1,)), ((), ())), preferred_element_type=F32)
        rhs_ref[...] = rhs[:rhs_ref.shape[0]] * (1.0 / times)

    cols = [f for _, f in build(lax.axis_index("reg") * 1048 + step * width, width)]
    gram = lax.dot_general(
        row_feat[...], jnp.concatenate(cols, axis=1), (((1,), (1,)), ((), ())), preferred_element_type=F32
    )
    gram_ref[...] = gram[:gram_ref.shape[0]] * (1.0 / times)


def per_device(snapshots, rates, basis):
    n, t = snapshots.shape
    rank = basis.shape[1]
    assert rank == 128 and t == 256 and n % CHUNKS == 0
    assert lax.axis_size("rows") == 16 and lax.axis_size("reg") == 8
    width = rank + rank * (rank + 1) // 2
    dma = pltpu.SemaphoreType.DMA
    states, moments = pl.pallas_call(
        exchange_kernel,
        out_shape=(
            jax.ShapeDtypeStruct((2, 64, 8, 256), F32),
            jax.ShapeDtypeStruct((2, 64, 16, 128), BF16),
        ),
        in_specs=[pl.BlockSpec(memory_space=pl.ANY)] * 3,
        out_specs=[pl.BlockSpec(memory_space=pltpu.VMEM)] * 2,
        scratch_shapes=[
            pltpu.VMEM((n, t), BF16),
            pltpu.VMEM((n, t), BF16),
            pltpu.VMEM((n, rank), BF16),
            pltpu.VMEM((rank, n), BF16),
            pltpu.VMEM((16, 8, 256), F32),
            pltpu.VMEM((16, 16, 128), F32),
            pltpu.VMEM((15, 8, 256), F32),
            pltpu.VMEM((15, 16, 128), F32),
            dma((3, CHUNKS)),
            dma((15,)), dma((15,)), dma((15,)), dma((15,)),
            dma((34,)), dma((34,)), dma((34,)), dma((34,)),
        ],
        compiler_params=pltpu.CompilerParams(collective_id=0, has_side_effects=True, vmem_limit_bytes=32 << 20),
        name="exchange",
    )(snapshots, rates, basis)
    row_width, col_width = width // 16, width // 8
    return pl.pallas_call(
        gram_kernel,
        grid=(pl.cdiv(col_width, 256),),
        out_shape=(
            jax.ShapeDtypeStruct((row_width, col_width), F32),
            jax.ShapeDtypeStruct((row_width, rank), F32),
        ),
        in_specs=[
            pl.BlockSpec((2, 64, 8, 256), lambda i: (0, 0, 0, 0)),
            pl.BlockSpec((2, 64, 16, 128), lambda i: (0, 0, 0, 0)),
        ],
        out_specs=[
            pl.BlockSpec((row_width, 256), lambda i: (0, i)),
            pl.BlockSpec((row_width, rank), lambda i: (0, 0)),
        ],
        scratch_shapes=[
            pltpu.VMEM((2 * rank, 8 * t), BF16),
            pltpu.VMEM((rank, 8 * t), BF16),
            pltpu.VMEM((pl.cdiv(row_width, 16) * 16, 8 * t), BF16),
        ],
        compiler_params=pltpu.CompilerParams(vmem_limit_bytes=48 << 20),
        name="gram",
    )(states, moments)


def solution(mesh):
    return jax.shard_map(
        per_device,
        mesh=mesh,
        in_specs=(P("rows", "reg"), P("rows", "reg"), P("rows", None)),
        out_specs=(P("rows", "reg"), P("rows", None)),
        check_vma=False,
    )
```

```python
import jax
import jax.numpy as jnp
from jax import lax
from jax.experimental import pallas as pl
from jax.experimental.pallas import tpu as pltpu
from jax.sharding import PartitionSpec as P

MESH = pl.DeviceIdType.MESH
F32 = jnp.float32
BF16 = jnp.bfloat16
CHUNKS = 4
VMEM_KIB = 47000


def device_at(x, y, z, c):
    return ((y * 2 + lax.rem(z, 2)) * 2 + c, lax.div(z, 2) * 4 + x)


def one_hot(base, count):
    rank = 128
    k = lax.broadcasted_iota(jnp.int32, (count, rank), 0) + base
    t = lax.broadcasted_iota(jnp.int32, (count, rank), 1)
    start = rank + t * rank - lax.div(t * (t - 1), 2)
    quad_i = (k >= start) & (k < start + rank - t)
    offset = jnp.sum(jnp.where(quad_i, t - start, 0).astype(F32), axis=1, keepdims=True)
    linear = k < rank
    pick_i = jnp.where(quad_i | (linear & (t == k)), 1.0, 0.0).astype(BF16)
    pick_j = jnp.where(((t - k).astype(F32) == offset) & (k >= rank), 1.0, 0.0).astype(BF16)
    return pick_i, pick_j


def exchange_kernel(
    snap_hbm, rates_hbm, basis_hbm, gram_out, row_out, moments_out,
    states, moments, row_feat, col_feat, acc, gram, snap, rates, basis, basis_t, part_s, part_m, land_s, land_m, pick_i, pick_j,
    load_sem, send_s, recv_s, send_m, recv_m,
    sg_send, sg_recv, mg_send, mg_recv, out_sem,
):
    rows, reg = lax.axis_index("rows"), lax.axis_index("reg")
    c = lax.rem(rows, 2)
    zl = lax.rem(lax.div(rows, 2), 2)
    y = lax.div(rows, 4)
    x = lax.rem(reg, 4)
    zh = lax.div(reg, 4)
    z = zh * 2 + zl
    twin = device_at(x, y, z, 1 - c)

    def turn(v, d):
        return lax.rem(v + d, 4)

    group = [(dy, dz, dc) for dy in range(4) for dz in range(2) for dc in range(2)][1:]

    def group_row(dy, dz, dc):
        return (turn(y, dy) * 2 + lax.rem(zl + dz, 2)) * 2 + lax.rem(c + dc, 2)

    depth = snap_hbm.shape[0] // CHUNKS
    loads = {}
    for i, k in [(i, k) for k in range(CHUNKS) for i in (0, 1)] + [(2, k) for k in range(CHUNKS)]:
        at = pl.ds(k * depth, depth)
        src, dst = ((basis_hbm, basis), (snap_hbm, snap), (rates_hbm, rates))[i]
        loads[i, k] = pltpu.make_async_copy(src.at[at, :], dst.at[at, :], load_sem.at[i, k])
        loads[i, k].start()

    barrier = pltpu.get_barrier_semaphore()
    with jax.named_scope("signal"):
        for dy, dz, dc in group:
            pl.semaphore_signal(barrier, inc=1, device_id=(group_row(dy, dz, dc), reg), device_id_type=MESH)
        for d in (1, 2, 3):
            pl.semaphore_signal(barrier, inc=1, device_id=device_at(turn(x, d), y, z, c), device_id_type=MESH)
        for d in (2, 3 + 2 * zl):
            pl.semaphore_signal(barrier, inc=1, device_id=device_at(x, y, turn(z, d), c), device_id_type=MESH)

    def all_of(ref, send, recv):
        return pltpu.make_async_remote_copy(
            src_ref=ref, dst_ref=ref, send_sem=send, recv_sem=recv, device_id=twin, device_id_type=MESH
        )

    def scatter(part, land, send, recv):
        for n, (dy, dz, dc) in enumerate(group):
            to = group_row(dy, dz, dc)
            pltpu.make_async_remote_copy(
                src_ref=part.at[to], dst_ref=land.at[n], send_sem=send, recv_sem=recv,
                device_id=(to, reg), device_id_type=MESH,
            ).start()

    def collect(part, land, send, recv):
        all_of(land, send, recv).wait_recv()
        piece = part[rows]
        for n in range(15):
            piece += land[n]
        return piece

    with jax.named_scope("proj_s"):
        total = jnp.zeros((128, 256), F32)
        for k in range(CHUNKS):
            at = pl.ds(k * depth, depth)
            loads[0, k].wait()
            loads[1, k].wait()
            turned = basis[at, :].T
            basis_t[:, at] = turned
            total += jnp.dot(turned, snap[at, :], preferred_element_type=F32)
        part_s[...] = total.T.reshape(16, 16, 128)
    with jax.named_scope("barrier_wait"):
        pl.semaphore_wait(barrier, 20)
    with jax.named_scope("send_s"):
        scatter(part_s, land_s, send_s, recv_s)
    with jax.named_scope("proj_m"):
        total = jnp.zeros((128, 256), F32)
        for k in range(CHUNKS):
            at = pl.ds(k * depth, depth)
            loads[2, k].wait()
            total += jnp.dot(basis_t[:, at], rates[at, :], preferred_element_type=F32)
        part_m[...] = total.T.reshape(16, 16, 128)
    with jax.named_scope("send_m"):
        scatter(part_m, land_m, send_m, recv_m)

    height, width = row_feat.shape[0], col_feat.shape[0]
    row_base, col_base = rows * 524, reg * 1048
    with jax.named_scope("picks"):
        for at, base, count in ((0, row_base, height), (height, col_base, width)):
            pick_i[at:at + count, :], pick_j[at:at + count, :] = one_hot(base, count)

    first = (1 - c) * y + c * z
    second = (1 - c) * z + c * x
    third = (1 - c) * x + c * y
    t_second = c * z + (1 - c) * x
    t_third = c * x + (1 - c) * y

    def peer(stage, d):
        step0, step1 = (1 - c) * d, c * d
        if stage == 1:
            return device_at(x, turn(y, step0), turn(z, step1), c)
        if stage == 2:
            return device_at(turn(x, step1), y, turn(z, step0), c)
        return device_at(turn(x, step0), turn(y, step1), z, c)

    own = (third * 4 + second) * 4 + first

    def quad(a3, a2):
        return pl.ds((a3 * 4 + a2) * 4, 4)

    def gather(buf, send, recv):
        flat = buf.reshape(128, *buf.shape[2:])

        def push(at, device, n):
            pltpu.make_async_remote_copy(
                src_ref=buf.at[c, at], dst_ref=buf.at[c, at], send_sem=send, recv_sem=recv.at[n],
                device_id=device, device_id_type=MESH,
            ).start()

        def arrive(core, at, n):
            all_of(buf.at[core, at], send, recv.at[n]).wait_recv()

        def stage1():
            for d in (1, 3, 2):
                push(pl.ds(own, 1), peer(1, d), 0)

        def stage2():
            arrive(c, pl.ds(0, 3), 0)
            mine = quad(third, second)
            for d in (2, 1, 3):
                push(mine, peer(2, d), d)
            for d in (1, 3, 2):
                push(mine, peer(3, d), 3 + d)

        def stage3():
            for e in (1, 3, 2):
                at = quad(third, turn(second, 4 - e))
                arrive(c, at, e)
                for d in (2, 1, 3):
                    push(at, peer(3, d), 3 + d)
            push(pl.ds(third * 16, 16), twin, 7)

        def from_afar(d):
            at = pl.ds(turn(third, 4 - d) * 16, 16)
            arrive(c, at, 3 + d)
            push(at, twin, 7 + d)

        def from_twin(d):
            arrive(1 - c, pl.ds(turn(t_third, 4 - d) * 16, 16), 7 + d)

        def drain():
            all_of(flat.at[pl.ds(0, 127)], send, recv.at[0]).wait_send()

        return stage1, stage2, stage3, from_afar, from_twin, drain

    s1, s2, s3, s_afar, s_twin, s_drain = gather(states, sg_send, sg_recv)
    m1, m2, m3, m_afar, m_twin, m_drain = gather(moments, mg_send, mg_recv)

    def features(core, a3, n):
        s = states[core, pl.ds(a3 * 16, 16)].reshape(256, 128)
        hi = s.astype(BF16)
        lo = (s - hi.astype(F32)).astype(BF16)
        split = jnp.concatenate([hi, lo], axis=1)

        def select(pick, at, count):
            e = pick[at:at + count, :]
            return lax.dot_general(
                jnp.concatenate([e, e], axis=1), split, (((1,), (1,)), ((), ())), preferred_element_type=F32
            )

        for out, at, base, slot in ((row_feat, 0, row_base, n), (col_feat, height, col_base, n % 2)):
            cols = slice(slot * 256, (slot + 1) * 256)
            k = lax.broadcasted_iota(jnp.int32, (128, 256), 0) + base
            plus = jnp.where(k < 128, 1.0, 0.0)
            count = out.shape[0]
            a, b = select(pick_i, at, count), select(pick_j, at, count)
            out[:128, cols] = (a[:128] * (b[:128] + plus)).astype(BF16)
            out[128:, cols] = (a[128:] * b[128:]).astype(BF16)
        cols = slice(n * 256, (n + 1) * 256)
        pltpu.make_async_copy(row_feat.at[:, cols], row_out.at[:, cols], out_sem.at[0]).start()

    times = row_feat.shape[1]
    out_rows, out_cols = gram.shape
    outs = [(row_feat, row_out, 0), (gram, gram_out, 1), (moments, moments_out, 2)]

    def accumulate(pair):
        lhs = row_feat[:, pair * 512:(pair + 1) * 512]
        for at in range(0, width, 256):
            to = min(at + 256, width)
            part = lax.dot_general(
                lhs, col_feat[at:to, :], (((1,), (1,)), ((), ())), preferred_element_type=F32
            )
            if pair:
                part += acc[:, at:to]
            if pair < times // 512 - 1:
                acc[:, at:to] = part
            else:
                to = min(to, out_cols)
                gram[:, at:to] = part[:out_rows, :to - at] * (1.0 / times)

    with jax.named_scope("rs_s"):
        states[c, own] = collect(part_s, land_s, send_s, recv_s)
    s1()
    with jax.named_scope("s2"):
        s2()
    with jax.named_scope("s3"):
        s3()
    with jax.named_scope("rs_m"):
        moments[c, own] = collect(part_m, land_m, send_m, recv_m).astype(BF16)
        m1()
    for n, d in enumerate((0, 1, 3, 2)):
        if d:
            with jax.named_scope(f"a{n}"):
                s_afar(d)
        with jax.named_scope(f"fa{n}"):
            features(c, turn(third, 4 - d), 2 * n)
        with jax.named_scope(f"t{n}"):
            s_twin(d)
        with jax.named_scope(f"ft{n}"):
            features(1 - c, turn(t_third, 4 - d), 2 * n + 1)
        with jax.named_scope(f"m{n}"):
            (m2, m3, lambda: m_afar(1), lambda: [m_afar(3), m_afar(2)])[n]()
        with jax.named_scope(f"g{n}"):
            accumulate(n)
    pltpu.make_async_copy(gram, gram_out, out_sem.at[1]).start()
    with jax.named_scope("m_twin"):
        for d in range(4):
            m_twin(d)
    pltpu.make_async_copy(moments, moments_out, out_sem.at[2]).start()
    with jax.named_scope("drain"):
        all_of(land_s, send_s, recv_s).wait_send()
        all_of(land_m, send_m, recv_m).wait_send()
        s_drain()
        m_drain()
        for src, dst, n in outs:
            pltpu.make_async_copy(src, dst, out_sem.at[n]).wait()


def finish_kernel(gram_ref, row_ref, moments_ref, gram_out, rhs_out, rhs_ref, sem):
    copy = pltpu.make_async_copy(gram_ref, gram_out, sem.at[0])
    copy.start()
    times = row_ref.shape[1]
    rows, reg = lax.axis_index("rows"), lax.axis_index("reg")
    c = lax.rem(rows, 2)
    y, x = lax.div(rows, 4), lax.rem(reg, 4)
    blocks = []
    for n, (d, far) in enumerate((d, far) for d in (0, 1, 3, 2) for far in (0, 1)):
        core = lax.rem(c + far, 2)
        a3 = lax.rem((1 - core) * x + core * y + 4 - d, 4)
        blocks.append(moments_ref[core, pl.ds(a3 * 16, 16)].reshape(256, 128))
    with jax.named_scope("rhs"):
        rhs = jnp.dot(row_ref[...], jnp.concatenate(blocks, axis=0), preferred_element_type=F32)
        rhs_ref[...] = rhs[:rhs_ref.shape[0]] * (1.0 / times)
    with jax.named_scope("k2wait"):
        rhs_copy = pltpu.make_async_copy(rhs_ref, rhs_out, sem.at[1])
        rhs_copy.start()
        copy.wait()
        rhs_copy.wait()


def per_device(snapshots, rates, basis):
    n, t = snapshots.shape
    rank = basis.shape[1]
    width = rank + rank * (rank + 1) // 2
    assert rank == 128 and t == 256 and n % CHUNKS == 0
    assert lax.axis_size("rows") == 16 and lax.axis_size("reg") == 8
    row_width, col_width = width // 16, width // 8
    row_pad, col_pad = pl.cdiv(row_width, 16) * 16, pl.cdiv(col_width, 16) * 16
    dma = pltpu.SemaphoreType.DMA
    gram, row_feat, moments = pl.pallas_call(
        exchange_kernel,
        out_shape=(
            jax.ShapeDtypeStruct((row_width, col_width), F32),
            jax.ShapeDtypeStruct((row_pad, 8 * t), BF16),
            jax.ShapeDtypeStruct((2, 64, 16, rank), BF16),
        ),
        in_specs=[pl.BlockSpec(memory_space=pl.ANY)] * 3,
        out_specs=[pl.BlockSpec(memory_space=pl.ANY)] * 3,
        scratch_shapes=[
            pltpu.VMEM((2, 64, 16, rank), F32),
            pltpu.VMEM((2, 64, 16, rank), BF16),
            pltpu.VMEM((row_pad, 8 * t), BF16),
            pltpu.VMEM((col_pad, 2 * t), BF16),
            pltpu.VMEM((row_pad, col_pad), F32),
            pltpu.VMEM((row_width, col_width), F32),
            pltpu.VMEM((n, t), BF16),
            pltpu.VMEM((n, t), BF16),
            pltpu.VMEM((n, rank), BF16),
            pltpu.VMEM((rank, n), BF16),
            pltpu.VMEM((16, 16, rank), F32),
            pltpu.VMEM((16, 16, rank), F32),
            pltpu.VMEM((15, 16, rank), F32),
            pltpu.VMEM((15, 16, rank), F32),
            pltpu.VMEM((row_pad + col_pad, rank), BF16),
            pltpu.VMEM((row_pad + col_pad, rank), BF16),
            dma((3, CHUNKS)),
            dma, dma, dma, dma,
            dma, dma((11,)), dma, dma((11,)), dma((3,)),
        ],
        compiler_params=pltpu.CompilerParams(
            collective_id=0, has_side_effects=True, vmem_limit_bytes=VMEM_KIB << 10
        ),
        name="exchange",
    )(*[pltpu.with_memory_space_constraint(a, pltpu.MemorySpace.HBM) for a in (snapshots, rates, basis)])
    return pl.pallas_call(
        finish_kernel,
        out_shape=(
            jax.ShapeDtypeStruct((row_width, col_width), F32),
            jax.ShapeDtypeStruct((row_width, rank), F32),
        ),
        in_specs=[
            pl.BlockSpec(memory_space=pl.ANY),
            pl.BlockSpec(memory_space=pltpu.VMEM),
            pl.BlockSpec(memory_space=pltpu.VMEM),
        ],
        out_specs=[pl.BlockSpec(memory_space=pl.ANY)] * 2,
        scratch_shapes=[pltpu.VMEM((row_width, rank), F32), dma((2,))],
        compiler_params=pltpu.CompilerParams(vmem_limit_bytes=16 << 20),
        name="finish",
    )(gram, row_feat, moments)


def solution(mesh):
    return jax.shard_map(
        per_device,
        mesh=mesh,
        in_specs=(P("rows", "reg"), P("rows", "reg"), P("rows", None)),
        out_specs=(P("rows", "reg"), P("rows", None)),
        check_vma=False,
    )
```

```python
import jax
import jax.numpy as jnp
from jax import lax
from jax.experimental import pallas as pl
from jax.experimental.pallas import tpu as pltpu
from jax.sharding import PartitionSpec as P

MESH = pl.DeviceIdType.MESH
F32 = jnp.float32
BF16 = jnp.bfloat16
CHUNKS = 4
VMEM_KIB = 47000


def device_at(x, y, z, c):
    return ((y * 2 + lax.rem(z, 2)) * 2 + c, lax.div(z, 2) * 4 + x)


def one_hot(base, count):
    rank = 128
    k = lax.broadcasted_iota(jnp.int32, (count, rank), 0) + base
    t = lax.broadcasted_iota(jnp.int32, (count, rank), 1)
    start = rank + t * rank - lax.div(t * (t - 1), 2)
    quad_i = (k >= start) & (k < start + rank - t)
    offset = jnp.sum(jnp.where(quad_i, t - start, 0).astype(F32), axis=1, keepdims=True)
    linear = k < rank
    pick_i = jnp.where(quad_i | (linear & (t == k)), 1.0, 0.0).astype(BF16)
    pick_j = jnp.where(((t - k).astype(F32) == offset) & (k >= rank), 1.0, 0.0).astype(BF16)
    return pick_i, pick_j


def exchange_kernel(
    snap_hbm, rates_hbm, basis_hbm, gram_out, row_out, moments_out,
    states, moments, row_feat, col_feat, acc, gram, snap, rates, basis, basis_t, part_s, part_m, land_s, land_m, pick_i, pick_j,
    load_sem, send_s, recv_s, send_m, recv_m,
    sg_send, sg_recv, mg_send, mg_recv, out_sem,
):
    rows, reg = lax.axis_index("rows"), lax.axis_index("reg")
    c = lax.rem(rows, 2)
    zl = lax.rem(lax.div(rows, 2), 2)
    y = lax.div(rows, 4)
    x = lax.rem(reg, 4)
    zh = lax.div(reg, 4)
    z = zh * 2 + zl
    twin = device_at(x, y, z, 1 - c)

    def turn(v, d):
        return lax.rem(v + d, 4)

    group = [(dy, dz, dc) for dy in range(4) for dz in range(2) for dc in range(2)][1:]
    chips = sorted(
        ((dx, dy, dz) for dx in range(4) for dy in range(4) for dz in range(4)),
        key=lambda d: (sum(min(a, 4 - a) for a in d), d),
    )
    xs, ys, zs = ([turn(v, d) for d in range(4)] for v in (x, y, z))

    def group_row(dy, dz, dc):
        return (ys[dy] * 2 + lax.rem(zl + dz, 2)) * 2 + lax.rem(c + dc, 2)

    def chip(dx, dy, dz):
        return device_at(xs[dx], ys[dy], zs[dz], c)

    depth = snap_hbm.shape[0] // CHUNKS
    loads = {}
    for i, k in [(i, k) for k in range(CHUNKS) for i in (0, 1)] + [(2, k) for k in range(CHUNKS)]:
        at = pl.ds(k * depth, depth)
        src, dst = ((basis_hbm, basis), (snap_hbm, snap), (rates_hbm, rates))[i]
        loads[i, k] = pltpu.make_async_copy(src.at[at, :], dst.at[at, :], load_sem.at[i, k])
        loads[i, k].start()

    barrier = pltpu.get_barrier_semaphore()
    with jax.named_scope("signal"):
        for dy, dz, dc in group:
            if dc:
                pl.semaphore_signal(barrier, inc=1, device_id=(group_row(dy, dz, dc), reg), device_id_type=MESH)
        for d in chips[1:]:
            pl.semaphore_signal(barrier, inc=1, device_id=chip(*d), device_id_type=MESH)

    def all_of(ref, send, recv):
        return pltpu.make_async_remote_copy(
            src_ref=ref, dst_ref=ref, send_sem=send, recv_sem=recv, device_id=twin, device_id_type=MESH
        )

    def scatter(part, land, send, recv):
        for n, (dy, dz, dc) in enumerate(group):
            to = group_row(dy, dz, dc)
            pltpu.make_async_remote_copy(
                src_ref=part.at[to], dst_ref=land.at[n], send_sem=send, recv_sem=recv,
                device_id=(to, reg), device_id_type=MESH,
            ).start()

    def collect(part, land, send, recv):
        all_of(land, send, recv).wait_recv()
        piece = part[rows]
        for n in range(15):
            piece += land[n]
        return piece

    with jax.named_scope("proj_s"):
        total = jnp.zeros((128, 256), F32)
        for k in range(CHUNKS):
            at = pl.ds(k * depth, depth)
            loads[0, k].wait()
            loads[1, k].wait()
            turned = basis[at, :].T
            basis_t[:, at] = turned
            total += jnp.dot(turned, snap[at, :], preferred_element_type=F32)
        part_s[...] = total.T.reshape(16, 16, 128)
    with jax.named_scope("barrier_wait"):
        pl.semaphore_wait(barrier, 71)
    with jax.named_scope("send_s"):
        scatter(part_s, land_s, send_s, recv_s)
    with jax.named_scope("proj_m"):
        total = jnp.zeros((128, 256), F32)
        for k in range(CHUNKS):
            at = pl.ds(k * depth, depth)
            loads[2, k].wait()
            total += jnp.dot(basis_t[:, at], rates[at, :], preferred_element_type=F32)
        part_m[...] = total.T.reshape(16, 16, 128)
    with jax.named_scope("send_m"):
        scatter(part_m, land_m, send_m, recv_m)

    height, width = row_feat.shape[0], col_feat.shape[0]
    row_base, col_base = rows * 524, reg * 1048
    with jax.named_scope("picks"):
        for at, base, count in ((0, row_base, height), (height, col_base, width)):
            pick_i[at:at + count, :], pick_j[at:at + count, :] = one_hot(base, count)

    def gather(buf, send, recv):
        flat = buf.reshape(128, *buf.shape[2:])

        def scatter_out():
            for n, d in enumerate(chips[1:], 1):
                pltpu.make_async_remote_copy(
                    src_ref=buf.at[c, 0], dst_ref=buf.at[c, n], send_sem=send, recv_sem=recv.at[n // 16],
                    device_id=chip(*d), device_id_type=MESH,
                ).start()

        def arrive(n):
            at = pl.ds(n * 16, 16)
            all_of(buf.at[c, pl.ds(0, 15) if n == 0 else at], send, recv.at[n]).wait_recv()
            pltpu.make_async_remote_copy(
                src_ref=buf.at[c, at], dst_ref=buf.at[c, at], send_sem=send, recv_sem=recv.at[4 + n],
                device_id=twin, device_id_type=MESH,
            ).start()

        def from_twin(n):
            all_of(buf.at[1 - c, pl.ds(n * 16, 16)], send, recv.at[4 + n]).wait_recv()

        def drain():
            all_of(flat.at[pl.ds(0, 127)], send, recv.at[0]).wait_send()

        return scatter_out, arrive, from_twin, drain

    s_out, s_arrive, s_twin, s_drain = gather(states, sg_send, sg_recv)
    m_out, m_arrive, m_twin, m_drain = gather(moments, mg_send, mg_recv)

    def features(core, block, n):
        s = states[core, block * 16:(block + 1) * 16].reshape(256, 128)
        hi = s.astype(BF16)
        lo = (s - hi.astype(F32)).astype(BF16)
        split = jnp.concatenate([hi, lo], axis=1)

        def select(pick, at, count):
            e = pick[at:at + count, :]
            return lax.dot_general(
                jnp.concatenate([e, e], axis=1), split, (((1,), (1,)), ((), ())), preferred_element_type=F32
            )

        for out, at, base, slot in ((row_feat, 0, row_base, n), (col_feat, height, col_base, n % 2)):
            cols = slice(slot * 256, (slot + 1) * 256)
            k = lax.broadcasted_iota(jnp.int32, (128, 256), 0) + base
            plus = jnp.where(k < 128, 1.0, 0.0)
            count = out.shape[0]
            a, b = select(pick_i, at, count), select(pick_j, at, count)
            out[:128, cols] = (a[:128] * (b[:128] + plus)).astype(BF16)
            out[128:, cols] = (a[128:] * b[128:]).astype(BF16)
        cols = slice(n * 256, (n + 1) * 256)
        pltpu.make_async_copy(row_feat.at[:, cols], row_out.at[:, cols], out_sem.at[0]).start()

    times = row_feat.shape[1]
    out_rows, out_cols = gram.shape
    outs = [(row_feat, row_out, 0), (gram, gram_out, 1), (moments, moments_out, 2)]

    def accumulate(pair):
        lhs = row_feat[:, pair * 512:(pair + 1) * 512]
        for at in range(0, width, 256):
            to = min(at + 256, width)
            part = lax.dot_general(
                lhs, col_feat[at:to, :], (((1,), (1,)), ((), ())), preferred_element_type=F32
            )
            if pair:
                part += acc[:, at:to]
            if pair < times // 512 - 1:
                acc[:, at:to] = part
            else:
                to = min(to, out_cols)
                gram[:, at:to] = part[:out_rows, :to - at] * (1.0 / times)

    with jax.named_scope("rs_s"):
        states[c, 0] = collect(part_s, land_s, send_s, recv_s)
    with jax.named_scope("s_out"):
        s_out()
    with jax.named_scope("rs_m"):
        moments[c, 0] = collect(part_m, land_m, send_m, recv_m).astype(BF16)
    with jax.named_scope("m_out"):
        m_out()
    with jax.named_scope("a0"):
        s_arrive(0)
    for n in range(4):
        with jax.named_scope(f"fa{n}"):
            features(c, n, 2 * n)
        if n < 3:
            with jax.named_scope(f"a{n + 1}"):
                s_arrive(n + 1)
        else:
            with jax.named_scope("m_arrive"):
                for k in range(4):
                    m_arrive(k)
        with jax.named_scope(f"t{n}"):
            s_twin(n)
        with jax.named_scope(f"ft{n}"):
            features(1 - c, n, 2 * n + 1)
        with jax.named_scope(f"g{n}"):
            accumulate(n)
    pltpu.make_async_copy(gram, gram_out, out_sem.at[1]).start()
    with jax.named_scope("m_twin"):
        for k in range(4):
            m_twin(k)
    pltpu.make_async_copy(moments, moments_out, out_sem.at[2]).start()
    with jax.named_scope("drain"):
        all_of(land_s, send_s, recv_s).wait_send()
        all_of(land_m, send_m, recv_m).wait_send()
        s_drain()
        m_drain()
        for src, dst, n in outs:
            pltpu.make_async_copy(src, dst, out_sem.at[n]).wait()


def finish_kernel(gram_ref, row_ref, moments_ref, gram_out, rhs_out, rhs_ref, sem):
    copy = pltpu.make_async_copy(gram_ref, gram_out, sem.at[0])
    copy.start()
    times = row_ref.shape[1]
    c = lax.rem(lax.axis_index("rows"), 2)
    blocks = [moments_ref[core, n * 16:(n + 1) * 16].reshape(256, 128) for n in range(4) for core in (c, 1 - c)]
    with jax.named_scope("rhs"):
        rhs = jnp.dot(row_ref[...], jnp.concatenate(blocks, axis=0), preferred_element_type=F32)
        rhs_ref[...] = rhs[:rhs_ref.shape[0]] * (1.0 / times)
    with jax.named_scope("k2wait"):
        rhs_copy = pltpu.make_async_copy(rhs_ref, rhs_out, sem.at[1])
        rhs_copy.start()
        copy.wait()
        rhs_copy.wait()


def per_device(snapshots, rates, basis):
    n, t = snapshots.shape
    rank = basis.shape[1]
    width = rank + rank * (rank + 1) // 2
    assert rank == 128 and t == 256 and n % CHUNKS == 0
    assert lax.axis_size("rows") == 16 and lax.axis_size("reg") == 8
    row_width, col_width = width // 16, width // 8
    row_pad, col_pad = pl.cdiv(row_width, 16) * 16, pl.cdiv(col_width, 16) * 16
    dma = pltpu.SemaphoreType.DMA
    gram, row_feat, moments = pl.pallas_call(
        exchange_kernel,
        out_shape=(
            jax.ShapeDtypeStruct((row_width, col_width), F32),
            jax.ShapeDtypeStruct((row_pad, 8 * t), BF16),
            jax.ShapeDtypeStruct((2, 64, 16, rank), BF16),
        ),
        in_specs=[pl.BlockSpec(memory_space=pl.ANY)] * 3,
        out_specs=[pl.BlockSpec(memory_space=pl.ANY)] * 3,
        scratch_shapes=[
            pltpu.VMEM((2, 64, 16, rank), F32),
            pltpu.VMEM((2, 64, 16, rank), BF16),
            pltpu.VMEM((row_pad, 8 * t), BF16),
            pltpu.VMEM((col_pad, 2 * t), BF16),
            pltpu.VMEM((row_pad, col_pad), F32),
            pltpu.VMEM((row_width, col_width), F32),
            pltpu.VMEM((n, t), BF16),
            pltpu.VMEM((n, t), BF16),
            pltpu.VMEM((n, rank), BF16),
            pltpu.VMEM((rank, n), BF16),
            pltpu.VMEM((16, 16, rank), F32),
            pltpu.VMEM((16, 16, rank), F32),
            pltpu.VMEM((15, 16, rank), F32),
            pltpu.VMEM((15, 16, rank), F32),
            pltpu.VMEM((row_pad + col_pad, rank), BF16),
            pltpu.VMEM((row_pad + col_pad, rank), BF16),
            dma((3, CHUNKS)),
            dma, dma, dma, dma,
            dma, dma((8,)), dma, dma((8,)), dma((3,)),
        ],
        compiler_params=pltpu.CompilerParams(
            collective_id=0, has_side_effects=True, vmem_limit_bytes=VMEM_KIB << 10
        ),
        name="exchange",
    )(*[pltpu.with_memory_space_constraint(a, pltpu.MemorySpace.HBM) for a in (snapshots, rates, basis)])
    return pl.pallas_call(
        finish_kernel,
        out_shape=(
            jax.ShapeDtypeStruct((row_width, col_width), F32),
            jax.ShapeDtypeStruct((row_width, rank), F32),
        ),
        in_specs=[
            pl.BlockSpec(memory_space=pl.ANY),
            pl.BlockSpec(memory_space=pltpu.VMEM),
            pl.BlockSpec(memory_space=pltpu.VMEM),
        ],
        out_specs=[pl.BlockSpec(memory_space=pl.ANY)] * 2,
        scratch_shapes=[pltpu.VMEM((row_width, rank), F32), dma((2,))],
        compiler_params=pltpu.CompilerParams(vmem_limit_bytes=16 << 20),
        name="finish",
    )(gram, row_feat, moments)


def solution(mesh):
    return jax.shard_map(
        per_device,
        mesh=mesh,
        in_specs=(P("rows", "reg"), P("rows", "reg"), P("rows", None)),
        out_specs=(P("rows", "reg"), P("rows", None)),
        check_vma=False,
    )
```

```python
import jax
import jax.numpy as jnp
from jax import lax
from jax.experimental import pallas as pl
from jax.experimental.pallas import tpu as pltpu
from jax.sharding import PartitionSpec as P

MESH = pl.DeviceIdType.MESH
F32 = jnp.float32
BF16 = jnp.bfloat16
CHUNKS = (2048, 2048, 2048, 2048)
VMEM_KIB = 47000


def device_at(x, y, z, c):
    return ((y * 2 + lax.rem(z, 2)) * 2 + c, lax.div(z, 2) * 4 + x)


def one_hot(base, count):
    rank = 128
    k = lax.broadcasted_iota(jnp.int32, (count, rank), 0) + base
    t = lax.broadcasted_iota(jnp.int32, (count, rank), 1)
    start = rank + t * rank - lax.div(t * (t - 1), 2)
    quad_i = (k >= start) & (k < start + rank - t)
    offset = jnp.sum(jnp.where(quad_i, t - start, 0).astype(F32), axis=1, keepdims=True)
    linear = k < rank
    pick_i = jnp.where(quad_i | (linear & (t == k)), 1.0, 0.0).astype(BF16)
    pick_j = jnp.where(((t - k).astype(F32) == offset) & (k >= rank), 1.0, 0.0).astype(BF16)
    return pick_i, pick_j


def exchange_kernel(
    snap_hbm, rates_hbm, basis_hbm, gram_out, row_out, moments_out,
    states, moments, feat, acc, gram, snap, rates, basis, basis_t, part_s, part_m, land_s, land_m, pick_i, pick_j,
    load_sem, send_s, recv_s, send_m, recv_m,
    sg_send, sg_recv, mg_send, mg_recv, f_send, f_recv, out_sem, here,
):
    rows, reg = lax.axis_index("rows"), lax.axis_index("reg")
    c = lax.rem(rows, 2)
    zl = lax.rem(lax.div(rows, 2), 2)
    y = lax.div(rows, 4)
    x = lax.rem(reg, 4)
    zh = lax.div(reg, 4)
    z = zh * 2 + zl
    twin = device_at(x, y, z, 1 - c)

    def turn(v, d):
        return lax.rem(v + d, 4)

    group = [(dy, dz, dc) for dy in range(4) for dz in range(2) for dc in range(2)][1:]
    chips = sorted(
        ((dx, dy, dz) for dx in range(4) for dy in range(4) for dz in range(4)),
        key=lambda d: (sum(min(a, 4 - a) for a in d), d),
    )
    xs, ys, zs = ([turn(v, d) for d in range(4)] for v in (x, y, z))

    def group_row(dy, dz, dc):
        return (ys[dy] * 2 + lax.rem(zl + dz, 2)) * 2 + lax.rem(c + dc, 2)

    def chip(dx, dy, dz):
        return device_at(xs[dx], ys[dy], zs[dz], c)

    chunks = [pl.ds(sum(CHUNKS[:k]), depth) for k, depth in enumerate(CHUNKS)]
    loads = {}
    for i, k in [(i, k) for k in range(len(chunks)) for i in (0, 1)] + [(2, k) for k in range(len(chunks))]:
        at = chunks[k]
        src, dst = ((basis_hbm, basis), (snap_hbm, snap), (rates_hbm, rates))[i]
        loads[i, k] = pltpu.make_async_copy(src.at[at, :], dst.at[at, :], load_sem.at[i, k])
        loads[i, k].start()

    barrier = pltpu.get_barrier_semaphore()
    with jax.named_scope("signal"):
        for dy, dz, dc in group:
            pl.semaphore_signal(barrier, inc=1, device_id=(group_row(dy, dz, dc), reg), device_id_type=MESH)
        for dx in (1, 2, 3):
            pl.semaphore_signal(barrier, inc=1, device_id=chip(dx, 0, 0), device_id_type=MESH)
        across = chip(0, 0, 2)
        pl.semaphore_signal(barrier, inc=1, device_id=across, device_id_type=MESH)

    def all_of(ref, send, recv):
        return pltpu.make_async_remote_copy(
            src_ref=ref, dst_ref=ref, send_sem=send, recv_sem=recv, device_id=twin, device_id_type=MESH
        )

    def scatter(part, land, send, recv):
        for n, (dy, dz, dc) in sorted(enumerate(group), key=lambda p: -(min(p[1][0], 4 - p[1][0]) + p[1][1])):
            to = group_row(dy, dz, dc)
            pltpu.make_async_remote_copy(
                src_ref=part.at[to], dst_ref=land.at[n], send_sem=send, recv_sem=recv,
                device_id=(to, reg), device_id_type=MESH,
            ).start()

    def collect(part, land, send, recv):
        all_of(land, send, recv).wait_recv()
        piece = part[rows]
        for n in range(15):
            piece += land[n]
        return piece

    with jax.named_scope("proj_s"):
        total = jnp.zeros((128, 256), F32)
        for k, at in enumerate(chunks):
            loads[0, k].wait()
            loads[1, k].wait()
            turned = basis[at, :].T
            basis_t[:, at] = turned
            total += jnp.dot(turned, snap[at, :], preferred_element_type=F32)
        part_s[...] = total.T.reshape(16, 16, 128)
    with jax.named_scope("barrier_wait"):
        pl.semaphore_wait(barrier, 19)
    with jax.named_scope("send_s"):
        scatter(part_s, land_s, send_s, recv_s)
    for dx in (1, 2, 3):
        pl.semaphore_signal(here.at[0], inc=1, device_id=chip(dx, 0, 0), device_id_type=MESH)
    with jax.named_scope("proj_m"):
        total = jnp.zeros((128, 256), F32)
        for k, at in enumerate(chunks):
            loads[2, k].wait()
            total += jnp.dot(basis_t[:, at], rates[at, :], preferred_element_type=F32)
        part_m[...] = total.T.reshape(16, 16, 128)
    with jax.named_scope("here0"):
        pl.semaphore_wait(here.at[0], 3)
        pl.semaphore_signal(here.at[1], inc=1, device_id=across, device_id_type=MESH)
    with jax.named_scope("send_m"):
        scatter(part_m, land_m, send_m, recv_m)

    height, width = row_out.shape[2], acc.shape[1]
    bases = ((0, rows * 524, height), (height, reg * 1048, width), (height + width, (rows + 1 - 2 * c) * 524, height))
    with jax.named_scope("picks"):
        for at, base, count in bases:
            pick_i[at:at + count, :], pick_j[at:at + count, :] = one_hot(base, count)

    def far(a, b, v):
        return turn(v, (1 - c) * a + c * b)

    pairs = [(a, b) for a in range(4) for b in range(4)]
    far_x, far_y, far_z = ({p: far(*p, v) for p in pairs} for v in (x, y, z))

    def target(dx, dy, dz):
        return device_at(far_x[dx, dy], far_y[dy, dz], far_z[dz, dx], c)

    def gather(buf, send, recv):
        flat = buf.reshape(buf.shape[0] * buf.shape[1], *buf.shape[2:])

        def scatter_out(first, last):
            for n, d in list(enumerate(chips))[first:last]:
                pltpu.make_async_remote_copy(
                    src_ref=buf.at[c, 0], dst_ref=buf.at[c, n], send_sem=send, recv_sem=recv.at[n // 16 if n > 6 else 8],
                    device_id=target(*d), device_id_type=MESH,
                ).start()

        def arrive_near():
            all_of(buf.at[c, pl.ds(0, 6)], send, recv.at[8]).wait_recv()

        def arrive(n):
            all_of(buf.at[c, pl.ds(0, 9 if n == 0 else 16)], send, recv.at[n]).wait_recv()

        def pass_on(n):
            at = pl.ds(n * 16, 16)
            pltpu.make_async_remote_copy(
                src_ref=buf.at[c, at], dst_ref=buf.at[c, at], send_sem=send, recv_sem=recv.at[4 + n],
                device_id=twin, device_id_type=MESH,
            ).start()

        def from_twin(n):
            all_of(buf.at[1 - c, pl.ds(n * 16, 16)], send, recv.at[4 + n]).wait_recv()

        def drain(count):
            all_of(flat.at[pl.ds(0, count)], send, recv.at[0]).wait_send()

        return scatter_out, arrive_near, arrive, pass_on, from_twin, drain

    s_out, s_near, s_arrive, s_pass, s_twin, s_drain = gather(states, sg_send, sg_recv)
    m_out, m_near, m_arrive, m_pass, m_twin, m_drain = gather(moments, mg_send, mg_recv)

    def features(core, n, parts):
        s = states[core, n * 16:(n + 1) * 16].reshape(256, 128)
        hi = s.astype(BF16)
        lo = (s - hi.astype(F32)).astype(BF16)
        split = jnp.concatenate([hi, lo], axis=1)

        def select(pick, at, count):
            e = pick[at:at + count, :]
            return lax.dot_general(
                jnp.concatenate([e, e], axis=1), split, (((1,), (1,)), ((), ())), preferred_element_type=F32
            )

        for at, base, count in parts[::-1]:
            k = lax.broadcasted_iota(jnp.int32, (128, 256), 0) + base
            plus = jnp.where(k < 128, 1.0, 0.0)
            a, b = select(pick_i, at, count), select(pick_j, at, count)
            feat[core, n, at:at + 128, :] = (a[:128] * (b[:128] + plus)).astype(BF16)
            feat[core, n, at + 128:at + count, :] = (a[128:] * b[128:]).astype(BF16)
        for src, dst in ((pl.ds(height + width, height), pl.ds(0, height)), (pl.ds(height, width),) * 2)[:len(parts) // 3 * 2]:
            pltpu.make_async_remote_copy(
                src_ref=feat.at[c, n, src], dst_ref=feat.at[c, n, dst], send_sem=f_send, recv_sem=f_recv.at[n],
                device_id=twin, device_id_type=MESH,
            ).start()

    times = 8 * 256
    out_rows, out_cols = gram.shape
    shared = pl.ds(0, height + width)

    def accumulate(n):
        if n < 3:
            all_of(feat.at[1 - c, n, shared], f_send, f_recv.at[n]).wait_recv()
        for q in range(2):
            pltpu.make_async_copy(feat.at[q, n, pl.ds(0, height)], row_out.at[q, n], out_sem.at[0]).start()
        lhs = jnp.concatenate([feat[q, n, :height, :] for q in range(2)], axis=1)
        for at in range(0, width, 256):
            to = min(at + 256, width)
            rhs = jnp.concatenate([feat[q, n, height + at:height + to, :] for q in range(2)], axis=1)
            part = lax.dot_general(lhs, rhs, (((1,), (1,)), ((), ())), preferred_element_type=F32)
            if n:
                part += acc[:, at:to]
            if n < 3:
                acc[:, at:to] = part
            else:
                to = min(to, out_cols)
                gram[:, at:to] = part[:out_rows, :to - at] * (1.0 / times)

    outs = [(moments, moments_out, 2), (gram, gram_out, 1)]

    with jax.named_scope("rs_s"):
        states[c, 0] = collect(part_s, land_s, send_s, recv_s)
    with jax.named_scope("here1"):
        pl.semaphore_wait(here.at[1], 1)
    with jax.named_scope("s_out"):
        s_out(1, 32)

        @pl.when(c == 0)
        def _():
            s_out(32, 64)

    with jax.named_scope("near"):
        s_near()

    @pl.when(c == 1)
    def _():
        s_out(32, 64)

    for n in range(4):
        with jax.named_scope(f"a{n}"):
            s_arrive(n)
            if n == 3:
                s_pass(n)
        if n == 1:
            with jax.named_scope("m_out"):
                moments[c, 0] = collect(part_m, land_m, send_m, recv_m).astype(BF16)
                m_out(1, 64)
        with jax.named_scope(f"f{n}"):
            features(c, n, bases if n < 3 else bases[:2])
        if n:
            with jax.named_scope(f"g{n - 1}"):
                accumulate(n - 1)
    with jax.named_scope("t3"):
        s_twin(3)
    with jax.named_scope("ft3"):
        features(1 - c, 3, bases[:2])
    with jax.named_scope("m_arrive"):
        m_near()
        for n in range(4):
            m_arrive(n)
            m_pass(n)
    with jax.named_scope("g3"):
        accumulate(3)
    pltpu.make_async_copy(gram, gram_out, out_sem.at[1]).start()
    with jax.named_scope("m_twin"):
        for k in range(4):
            m_twin(k)
    pltpu.make_async_copy(moments, moments_out, out_sem.at[2]).start()
    with jax.named_scope("drain"):
        all_of(land_s, send_s, recv_s).wait_send()
        all_of(land_m, send_m, recv_m).wait_send()
        s_drain(79)
        m_drain(127)
        all_of(feat.at[c, pl.ds(0, 3), shared], f_send, f_recv.at[0]).wait_send()
        for src, dst, n in [(row_out, row_out, 0)] + outs:
            pltpu.make_async_copy(src, dst, out_sem.at[n]).wait()


def finish_kernel(gram_ref, row_ref, moments_ref, gram_out, rhs_out, rhs_ref, sem):
    copy = pltpu.make_async_copy(gram_ref, gram_out, sem.at[0])
    copy.start()
    blocks = [(q, n) for q in range(2) for n in range(4)]
    with jax.named_scope("rhs"):
        rhs = jnp.dot(
            jnp.concatenate([row_ref[q, n] for q, n in blocks], axis=1),
            jnp.concatenate([moments_ref[q, n * 16:(n + 1) * 16].reshape(256, 128) for q, n in blocks], axis=0),
            preferred_element_type=F32,
        )
        rhs_ref[...] = rhs[:rhs_ref.shape[0]] * (1.0 / (256 * len(blocks)))
    with jax.named_scope("k2wait"):
        rhs_copy = pltpu.make_async_copy(rhs_ref, rhs_out, sem.at[1])
        rhs_copy.start()
        copy.wait()
        rhs_copy.wait()


def per_device(snapshots, rates, basis):
    n, t = snapshots.shape
    rank = basis.shape[1]
    width = rank + rank * (rank + 1) // 2
    assert rank == 128 and t == 256 and n == sum(CHUNKS)
    assert lax.axis_size("rows") == 16 and lax.axis_size("reg") == 8
    row_width, col_width = width // 16, width // 8
    row_pad, col_pad = pl.cdiv(row_width, 16) * 16, pl.cdiv(col_width, 16) * 16
    dma = pltpu.SemaphoreType.DMA
    gram, row_feat, moments = pl.pallas_call(
        exchange_kernel,
        out_shape=(
            jax.ShapeDtypeStruct((row_width, col_width), F32),
            jax.ShapeDtypeStruct((2, 4, row_pad, t), BF16),
            jax.ShapeDtypeStruct((2, 64, 16, rank), BF16),
        ),
        in_specs=[pl.BlockSpec(memory_space=pl.ANY)] * 3,
        out_specs=[pl.BlockSpec(memory_space=pl.ANY)] * 3,
        scratch_shapes=[
            pltpu.VMEM((2, 64, 16, rank), F32),
            pltpu.VMEM((2, 64, 16, rank), BF16),
            pltpu.VMEM((2, 4, 2 * row_pad + col_pad, t), BF16),
            pltpu.VMEM((row_pad, col_pad), F32),
            pltpu.VMEM((row_width, col_width), F32),
            pltpu.VMEM((n, t), BF16),
            pltpu.VMEM((n, t), BF16),
            pltpu.VMEM((n, rank), BF16),
            pltpu.VMEM((rank, n), BF16),
            pltpu.VMEM((16, 16, rank), F32),
            pltpu.VMEM((16, 16, rank), F32),
            pltpu.VMEM((15, 16, rank), F32),
            pltpu.VMEM((15, 16, rank), F32),
            pltpu.VMEM((2 * row_pad + col_pad, rank), BF16),
            pltpu.VMEM((2 * row_pad + col_pad, rank), BF16),
            dma((3, len(CHUNKS))),
            dma, dma, dma, dma,
            dma, dma((9,)), dma, dma((9,)), dma, dma((3,)), dma((3,)), pltpu.SemaphoreType.REGULAR((2,)),
        ],
        compiler_params=pltpu.CompilerParams(
            collective_id=0, has_side_effects=True, vmem_limit_bytes=VMEM_KIB << 10
        ),
        name="exchange",
    )(*[pltpu.with_memory_space_constraint(a, pltpu.MemorySpace.HBM) for a in (snapshots, rates, basis)])
    return pl.pallas_call(
        finish_kernel,
        out_shape=(
            jax.ShapeDtypeStruct((row_width, col_width), F32),
            jax.ShapeDtypeStruct((row_width, rank), F32),
        ),
        in_specs=[
            pl.BlockSpec(memory_space=pl.ANY),
            pl.BlockSpec(memory_space=pltpu.VMEM),
            pl.BlockSpec(memory_space=pltpu.VMEM),
        ],
        out_specs=[pl.BlockSpec(memory_space=pl.ANY)] * 2,
        scratch_shapes=[pltpu.VMEM((row_width, rank), F32), dma((2,))],
        compiler_params=pltpu.CompilerParams(vmem_limit_bytes=16 << 20),
        name="finish",
    )(gram, row_feat, moments)


def solution(mesh):
    return jax.shard_map(
        per_device,
        mesh=mesh,
        in_specs=(P("rows", "reg"), P("rows", "reg"), P("rows", None)),
        out_specs=(P("rows", "reg"), P("rows", None)),
        check_vma=False,
    )
```

```python
import jax
import jax.numpy as jnp
from jax import lax
from jax.experimental import pallas as pl
from jax.experimental.pallas import tpu as pltpu
from jax.sharding import PartitionSpec as P

MESH = pl.DeviceIdType.MESH
F32 = jnp.float32
BF16 = jnp.bfloat16
CHUNKS = (2048, 2048, 2048, 2048)
VMEM_KIB = 47000


def device_at(x, y, z, c):
    return ((y * 2 + lax.rem(z, 2)) * 2 + c, lax.div(z, 2) * 4 + x)


def one_hot(base, count):
    rank = 128
    k = lax.broadcasted_iota(jnp.int32, (count, rank), 0) + base
    t = lax.broadcasted_iota(jnp.int32, (count, rank), 1)
    start = rank + t * rank - lax.div(t * (t - 1), 2)
    quad_i = (k >= start) & (k < start + rank - t)
    offset = jnp.sum(jnp.where(quad_i, t - start, 0).astype(F32), axis=1, keepdims=True)
    linear = k < rank
    pick_i = jnp.where(quad_i | (linear & (t == k)), 1.0, 0.0).astype(BF16)
    pick_j = jnp.where(((t - k).astype(F32) == offset) & (k >= rank), 1.0, 0.0).astype(BF16)
    return pick_i, pick_j


def exchange_kernel(
    snap_hbm, rates_hbm, basis_hbm, gram_out, row_out, moments_out,
    states, moments, feat, acc, gram, snap, rates, basis, basis_t, part_s, part_m, half_m, land_s, land_m, land_h, pick_i, pick_j,
    load_sem, send_s, recv_s, send_m, recv_m, send_h, recv_h,
    sg_send, sg_recv, mg_send, mg_recv, f_send, f_recv, out_sem, here,
):
    rows, reg = lax.axis_index("rows"), lax.axis_index("reg")
    c = lax.rem(rows, 2)
    zl = lax.rem(lax.div(rows, 2), 2)
    y = lax.div(rows, 4)
    x = lax.rem(reg, 4)
    zh = lax.div(reg, 4)
    z = zh * 2 + zl
    twin = device_at(x, y, z, 1 - c)

    def turn(v, d):
        return lax.rem(v + d, 4)

    group = [(dy, dz, dc) for dy in range(4) for dz in range(2) for dc in range(2)][1:]
    chips = sorted(
        ((dx, dy, dz) for dx in range(4) for dy in range(4) for dz in range(4)),
        key=lambda d: (sum(min(a, 4 - a) for a in d), d),
    )
    xs, ys, zs = ([turn(v, d) for d in range(4)] for v in (x, y, z))

    def group_row(dy, dz, dc):
        return (ys[dy] * 2 + lax.rem(zl + dz, 2)) * 2 + lax.rem(c + dc, 2)

    def chip(dx, dy, dz):
        return device_at(xs[dx], ys[dy], zs[dz], c)

    chunks = [pl.ds(sum(CHUNKS[:k]), depth) for k, depth in enumerate(CHUNKS)]
    loads = {}
    for i, k in [(i, k) for k in range(len(chunks)) for i in (0, 1)] + [(2, k) for k in range(len(chunks))]:
        at = chunks[k]
        src, dst = ((basis_hbm, basis), (snap_hbm, snap), (rates_hbm, rates))[i]
        loads[i, k] = pltpu.make_async_copy(src.at[at, :], dst.at[at, :], load_sem.at[i, k])
        loads[i, k].start()

    barrier = pltpu.get_barrier_semaphore()
    with jax.named_scope("signal"):
        for dy, dz, dc in group:
            pl.semaphore_signal(barrier, inc=1, device_id=(group_row(dy, dz, dc), reg), device_id_type=MESH)
        for dx in (1, 2, 3):
            pl.semaphore_signal(barrier, inc=1, device_id=chip(dx, 0, 0), device_id_type=MESH)
        across = chip(0, 0, 2)
        pl.semaphore_signal(barrier, inc=1, device_id=across, device_id_type=MESH)

    def all_of(ref, send, recv):
        return pltpu.make_async_remote_copy(
            src_ref=ref, dst_ref=ref, send_sem=send, recv_sem=recv, device_id=twin, device_id_type=MESH
        )

    def scatter(part, land, send, recv):
        for n, (dy, dz, dc) in sorted(enumerate(group), key=lambda p: -(min(p[1][0], 4 - p[1][0]) + p[1][1])):
            to = group_row(dy, dz, dc)
            pltpu.make_async_remote_copy(
                src_ref=part.at[to], dst_ref=land.at[n], send_sem=send, recv_sem=recv,
                device_id=(to, reg), device_id_type=MESH,
            ).start()

    pair = [d for d in group if not d[2]]

    def collect(part, at, land, send, recv):
        all_of(land, send, recv).wait_recv()
        piece = part[at]
        for n in range(land.shape[0]):
            piece += land[n]
        return piece

    with jax.named_scope("proj_s"):
        total = jnp.zeros((128, 256), F32)
        for k, at in enumerate(chunks):
            loads[0, k].wait()
            loads[1, k].wait()
            turned = basis[at, :].T
            basis_t[:, at] = turned
            total += jnp.dot(turned, snap[at, :], preferred_element_type=F32)
        part_s[...] = total.T.reshape(16, 16, 128)
    with jax.named_scope("barrier_wait"):
        pl.semaphore_wait(barrier, 19)
    with jax.named_scope("send_s"):
        scatter(part_s, land_s, send_s, recv_s)
    for dx in (1, 2, 3):
        pl.semaphore_signal(here.at[0], inc=1, device_id=chip(dx, 0, 0), device_id_type=MESH)
    with jax.named_scope("proj_m"):
        total = jnp.zeros((128, 256), F32)
        for k, at in enumerate(chunks):
            loads[2, k].wait()
            total += jnp.dot(basis_t[:, at], rates[at, :], preferred_element_type=F32)
        part_m[...] = total.T.reshape(8, 2, 16, 128)
    with jax.named_scope("here0"):
        pl.semaphore_wait(here.at[0], 3)
        pl.semaphore_signal(here.at[1], inc=1, device_id=across, device_id_type=MESH)
    with jax.named_scope("send_m"):
        pltpu.make_async_remote_copy(
            src_ref=part_m.at[:, 1 - c], dst_ref=land_h, send_sem=send_h, recv_sem=recv_h,
            device_id=twin, device_id_type=MESH,
        ).start()

    height, width = row_out.shape[2], acc.shape[1]
    bases = ((0, rows * 524, height), (height, reg * 1048, width), (height + width, (rows + 1 - 2 * c) * 524, height))
    with jax.named_scope("picks"):
        for at, base, count in bases:
            pick_i[at:at + count, :], pick_j[at:at + count, :] = one_hot(base, count)

    def far(a, b, v):
        return turn(v, (1 - c) * a + c * b)

    pairs = [(a, b) for a in range(4) for b in range(4)]
    far_x, far_y, far_z = ({p: far(*p, v) for p in pairs} for v in (x, y, z))

    def target(dx, dy, dz):
        return device_at(far_x[dx, dy], far_y[dy, dz], far_z[dz, dx], c)

    def gather(buf, send, recv):
        flat = buf.reshape(buf.shape[0] * buf.shape[1], *buf.shape[2:])

        def scatter_out(first, last):
            for n, d in list(enumerate(chips))[first:last]:
                pltpu.make_async_remote_copy(
                    src_ref=buf.at[c, 0], dst_ref=buf.at[c, n], send_sem=send, recv_sem=recv.at[n // 16 if n > 6 else 8],
                    device_id=target(*d), device_id_type=MESH,
                ).start()

        def arrive_near():
            all_of(buf.at[c, pl.ds(0, 6)], send, recv.at[8]).wait_recv()

        def arrive(n):
            all_of(buf.at[c, pl.ds(0, 9 if n == 0 else 16)], send, recv.at[n]).wait_recv()

        def pass_on(n):
            at = pl.ds(n * 16, 16)
            pltpu.make_async_remote_copy(
                src_ref=buf.at[c, at], dst_ref=buf.at[c, at], send_sem=send, recv_sem=recv.at[4 + n],
                device_id=twin, device_id_type=MESH,
            ).start()

        def from_twin(n):
            all_of(buf.at[1 - c, pl.ds(n * 16, 16)], send, recv.at[4 + n]).wait_recv()

        def drain(count):
            all_of(flat.at[pl.ds(0, count)], send, recv.at[0]).wait_send()

        return scatter_out, arrive_near, arrive, pass_on, from_twin, drain

    s_out, s_near, s_arrive, s_pass, s_twin, s_drain = gather(states, sg_send, sg_recv)
    m_out, m_near, m_arrive, m_pass, m_twin, m_drain = gather(moments, mg_send, mg_recv)

    def features(core, n, parts):
        s = states[core, n * 16:(n + 1) * 16].reshape(256, 128)
        hi = s.astype(BF16)
        lo = (s - hi.astype(F32)).astype(BF16)
        split = jnp.concatenate([hi, lo], axis=1)

        def select(pick, at, count):
            e = pick[at:at + count, :]
            return lax.dot_general(
                jnp.concatenate([e, e], axis=1), split, (((1,), (1,)), ((), ())), preferred_element_type=F32
            )

        for at, base, count in parts[::-1]:
            k = lax.broadcasted_iota(jnp.int32, (128, 256), 0) + base
            plus = jnp.where(k < 128, 1.0, 0.0)
            a, b = select(pick_i, at, count), select(pick_j, at, count)
            feat[core, n, at:at + 128, :] = (a[:128] * (b[:128] + plus)).astype(BF16)
            feat[core, n, at + 128:at + count, :] = (a[128:] * b[128:]).astype(BF16)
        for src, dst in ((pl.ds(height + width, height), pl.ds(0, height)), (pl.ds(height, width),) * 2)[:len(parts) // 3 * 2]:
            pltpu.make_async_remote_copy(
                src_ref=feat.at[c, n, src], dst_ref=feat.at[c, n, dst], send_sem=f_send, recv_sem=f_recv.at[n],
                device_id=twin, device_id_type=MESH,
            ).start()

    times = 8 * 256
    out_rows, out_cols = gram.shape
    shared = pl.ds(0, height + width)

    def accumulate(n):
        if n < 3:
            all_of(feat.at[1 - c, n, shared], f_send, f_recv.at[n]).wait_recv()
        for q in range(2):
            pltpu.make_async_copy(feat.at[q, n, pl.ds(0, height)], row_out.at[q, n], out_sem.at[0]).start()
        lhs = jnp.concatenate([feat[q, n, :height, :] for q in range(2)], axis=1)
        for at in range(0, width, 256):
            to = min(at + 256, width)
            rhs = jnp.concatenate([feat[q, n, height + at:height + to, :] for q in range(2)], axis=1)
            part = lax.dot_general(lhs, rhs, (((1,), (1,)), ((), ())), preferred_element_type=F32)
            if n:
                part += acc[:, at:to]
            if n < 3:
                acc[:, at:to] = part
            else:
                to = min(to, out_cols)
                gram[:, at:to] = part[:out_rows, :to - at] * (1.0 / times)

    outs = [(moments, moments_out, 2), (gram, gram_out, 1)]

    with jax.named_scope("half_m"):
        all_of(land_h, send_h, recv_h).wait_recv()
        half_m[...] = part_m[:, c] + land_h[...]
        for n, (dy, dz, _) in enumerate(pair):
            to = ys[dy] * 2 + lax.rem(zl + dz, 2)
            pltpu.make_async_remote_copy(
                src_ref=half_m.at[to], dst_ref=land_m.at[n], send_sem=send_m, recv_sem=recv_m,
                device_id=(to * 2 + c, reg), device_id_type=MESH,
            ).start()
    with jax.named_scope("rs_s"):
        states[c, 0] = collect(part_s, rows, land_s, send_s, recv_s)
    with jax.named_scope("here1"):
        pl.semaphore_wait(here.at[1], 1)
    with jax.named_scope("s_out"):
        s_out(1, 32)

        @pl.when(c == 0)
        def _():
            s_out(32, 64)

    with jax.named_scope("near"):
        s_near()

    @pl.when(c == 1)
    def _():
        s_out(32, 64)

    for n in range(4):
        if n == 1:
            with jax.named_scope("m_out"):
                moments[c, 0] = collect(half_m, lax.div(rows, 2), land_m, send_m, recv_m).astype(BF16)
                m_out(1, 64)
        with jax.named_scope(f"a{n}"):
            s_arrive(n)
            if n == 3:
                s_pass(n)
        with jax.named_scope(f"f{n}"):
            features(c, n, bases if n < 3 else bases[:2])
        if n:
            with jax.named_scope(f"g{n - 1}"):
                accumulate(n - 1)
    with jax.named_scope("t3"):
        s_twin(3)
    with jax.named_scope("ft3"):
        features(1 - c, 3, bases[:2])
    with jax.named_scope("m_arrive"):
        m_near()
        for n in range(4):
            m_arrive(n)
            m_pass(n)
    with jax.named_scope("g3"):
        accumulate(3)
    pltpu.make_async_copy(gram, gram_out, out_sem.at[1]).start()
    with jax.named_scope("m_twin"):
        for k in range(4):
            m_twin(k)
    pltpu.make_async_copy(moments, moments_out, out_sem.at[2]).start()
    with jax.named_scope("drain"):
        all_of(land_s, send_s, recv_s).wait_send()
        all_of(land_m, send_m, recv_m).wait_send()
        all_of(land_h, send_h, recv_h).wait_send()
        s_drain(79)
        m_drain(127)
        all_of(feat.at[c, pl.ds(0, 3), shared], f_send, f_recv.at[0]).wait_send()
        for src, dst, n in [(row_out, row_out, 0)] + outs:
            pltpu.make_async_copy(src, dst, out_sem.at[n]).wait()


def finish_kernel(gram_ref, row_ref, moments_ref, gram_out, rhs_out, rhs_ref, sem):
    copy = pltpu.make_async_copy(gram_ref, gram_out, sem.at[0])
    copy.start()
    blocks = [(q, n) for q in range(2) for n in range(4)]
    with jax.named_scope("rhs"):
        rhs = jnp.dot(
            jnp.concatenate([row_ref[q, n] for q, n in blocks], axis=1),
            jnp.concatenate([moments_ref[q, n * 16:(n + 1) * 16].reshape(256, 128) for q, n in blocks], axis=0),
            preferred_element_type=F32,
        )
        rhs_ref[...] = rhs[:rhs_ref.shape[0]] * (1.0 / (256 * len(blocks)))
    with jax.named_scope("k2wait"):
        rhs_copy = pltpu.make_async_copy(rhs_ref, rhs_out, sem.at[1])
        rhs_copy.start()
        copy.wait()
        rhs_copy.wait()


def per_device(snapshots, rates, basis):
    n, t = snapshots.shape
    rank = basis.shape[1]
    width = rank + rank * (rank + 1) // 2
    assert rank == 128 and t == 256 and n == sum(CHUNKS)
    assert lax.axis_size("rows") == 16 and lax.axis_size("reg") == 8
    row_width, col_width = width // 16, width // 8
    row_pad, col_pad = pl.cdiv(row_width, 16) * 16, pl.cdiv(col_width, 16) * 16
    dma = pltpu.SemaphoreType.DMA
    gram, row_feat, moments = pl.pallas_call(
        exchange_kernel,
        out_shape=(
            jax.ShapeDtypeStruct((row_width, col_width), F32),
            jax.ShapeDtypeStruct((2, 4, row_pad, t), BF16),
            jax.ShapeDtypeStruct((2, 64, 16, rank), BF16),
        ),
        in_specs=[pl.BlockSpec(memory_space=pl.ANY)] * 3,
        out_specs=[pl.BlockSpec(memory_space=pl.ANY)] * 3,
        scratch_shapes=[
            pltpu.VMEM((2, 64, 16, rank), F32),
            pltpu.VMEM((2, 64, 16, rank), BF16),
            pltpu.VMEM((2, 4, 2 * row_pad + col_pad, t), BF16),
            pltpu.VMEM((row_pad, col_pad), F32),
            pltpu.VMEM((row_width, col_width), F32),
            pltpu.VMEM((n, t), BF16),
            pltpu.VMEM((n, t), BF16),
            pltpu.VMEM((n, rank), BF16),
            pltpu.VMEM((rank, n), BF16),
            pltpu.VMEM((16, 16, rank), F32),
            pltpu.VMEM((8, 2, 16, rank), F32),
            pltpu.VMEM((8, 16, rank), F32),
            pltpu.VMEM((15, 16, rank), F32),
            pltpu.VMEM((7, 16, rank), F32),
            pltpu.VMEM((8, 16, rank), F32),
            pltpu.VMEM((2 * row_pad + col_pad, rank), BF16),
            pltpu.VMEM((2 * row_pad + col_pad, rank), BF16),
            dma((3, len(CHUNKS))),
            dma, dma, dma, dma, dma, dma,
            dma, dma((9,)), dma, dma((9,)), dma, dma((3,)), dma((3,)), pltpu.SemaphoreType.REGULAR((2,)),
        ],
        compiler_params=pltpu.CompilerParams(
            collective_id=0, has_side_effects=True, vmem_limit_bytes=VMEM_KIB << 10
        ),
        name="exchange",
    )(*[pltpu.with_memory_space_constraint(a, pltpu.MemorySpace.HBM) for a in (snapshots, rates, basis)])
    return pl.pallas_call(
        finish_kernel,
        out_shape=(
            jax.ShapeDtypeStruct((row_width, col_width), F32),
            jax.ShapeDtypeStruct((row_width, rank), F32),
        ),
        in_specs=[
            pl.BlockSpec(memory_space=pl.ANY),
            pl.BlockSpec(memory_space=pltpu.VMEM),
            pl.BlockSpec(memory_space=pltpu.VMEM),
        ],
        out_specs=[pl.BlockSpec(memory_space=pl.ANY)] * 2,
        scratch_shapes=[pltpu.VMEM((row_width, rank), F32), dma((2,))],
        compiler_params=pltpu.CompilerParams(vmem_limit_bytes=16 << 20),
        name="finish",
    )(gram, row_feat, moments)


def solution(mesh):
    return jax.shard_map(
        per_device,
        mesh=mesh,
        in_specs=(P("rows", "reg"), P("rows", "reg"), P("rows", None)),
        out_specs=(P("rows", "reg"), P("rows", None)),
        check_vma=False,
    )
```

```python
import jax
import jax.numpy as jnp
from jax import lax
from jax.experimental import pallas as pl
from jax.experimental.pallas import tpu as pltpu
from jax.sharding import PartitionSpec as P

MESH = pl.DeviceIdType.MESH
F32 = jnp.float32
BF16 = jnp.bfloat16
CHUNKS = (2048, 2048, 2048, 2048)
VMEM_KIB = 47000


def device_at(x, y, z, c):
    return ((y * 2 + lax.rem(z, 2)) * 2 + c, lax.div(z, 2) * 4 + x)


def one_hot(base, count):
    rank = 128
    k = lax.broadcasted_iota(jnp.int32, (count, rank), 0) + base
    t = lax.broadcasted_iota(jnp.int32, (count, rank), 1)
    start = rank + t * rank - lax.div(t * (t - 1), 2)
    quad_i = (k >= start) & (k < start + rank - t)
    offset = jnp.sum(jnp.where(quad_i, t - start, 0).astype(F32), axis=1, keepdims=True)
    linear = k < rank
    pick_i = jnp.where(quad_i | (linear & (t == k)), 1.0, 0.0).astype(BF16)
    pick_j = jnp.where(((t - k).astype(F32) == offset) & (k >= rank), 1.0, 0.0).astype(BF16)
    return pick_i, pick_j


def exchange_kernel(
    snap_hbm, rates_hbm, basis_hbm, gram_out, row_out, moments_out,
    states, moments, feat, acc, gram, snap, rates, basis, basis_t, part_s, part_m, half_m, land_s, land_m, land_h, pick_i, pick_j,
    load_sem, send_s, recv_s, send_m, recv_m, send_h, recv_h,
    sg_send, sg_recv, mg_send, mg_recv, f_send, f_recv, out_sem, here,
):
    rows, reg = lax.axis_index("rows"), lax.axis_index("reg")
    c = lax.rem(rows, 2)
    zl = lax.rem(lax.div(rows, 2), 2)
    y = lax.div(rows, 4)
    x = lax.rem(reg, 4)
    zh = lax.div(reg, 4)
    z = zh * 2 + zl
    twin = device_at(x, y, z, 1 - c)

    def turn(v, d):
        return lax.rem(v + d, 4)

    group = [(dy, dz, dc) for dy in range(4) for dz in range(2) for dc in range(2)][1:]
    chips = sorted(
        ((dx, dy, dz) for dx in range(4) for dy in range(4) for dz in range(4)),
        key=lambda d: (sum(min(a, 4 - a) for a in d), d),
    )
    xs, ys, zs = ([turn(v, d) for d in range(4)] for v in (x, y, z))

    def group_row(dy, dz, dc):
        return (ys[dy] * 2 + lax.rem(zl + dz, 2)) * 2 + lax.rem(c + dc, 2)

    def chip(dx, dy, dz):
        return device_at(xs[dx], ys[dy], zs[dz], c)

    chunks = [pl.ds(sum(CHUNKS[:k]), depth) for k, depth in enumerate(CHUNKS)]
    loads = {}
    for i, k in [(i, k) for k in range(len(chunks)) for i in (0, 1)] + [(2, k) for k in range(len(chunks))]:
        at = chunks[k]
        src, dst = ((basis_hbm, basis), (snap_hbm, snap), (rates_hbm, rates))[i]
        loads[i, k] = pltpu.make_async_copy(src.at[at, :], dst.at[at, :], load_sem.at[i, k])
        loads[i, k].start()

    barrier = pltpu.get_barrier_semaphore()
    with jax.named_scope("signal"):
        for dy, dz, dc in group:
            pl.semaphore_signal(barrier, inc=1, device_id=(group_row(dy, dz, dc), reg), device_id_type=MESH)
        for dx in (1, 2, 3):
            pl.semaphore_signal(barrier, inc=1, device_id=chip(dx, 0, 0), device_id_type=MESH)
        across = chip(0, 0, 2)
        pl.semaphore_signal(barrier, inc=1, device_id=across, device_id_type=MESH)

    def all_of(ref, send, recv):
        return pltpu.make_async_remote_copy(
            src_ref=ref, dst_ref=ref, send_sem=send, recv_sem=recv, device_id=twin, device_id_type=MESH
        )

    def scatter(part, land, send, recv):
        for n, (dy, dz, dc) in sorted(enumerate(group), key=lambda p: -(min(p[1][0], 4 - p[1][0]) + p[1][1])):
            to = group_row(dy, dz, dc)
            pltpu.make_async_remote_copy(
                src_ref=part.at[to], dst_ref=land.at[n], send_sem=send, recv_sem=recv,
                device_id=(to, reg), device_id_type=MESH,
            ).start()

    pair = [d for d in group if not d[2]]

    def collect(part, at, land, send, recv):
        all_of(land, send, recv).wait_recv()
        piece = part[at]
        for n in range(land.shape[0]):
            piece += land[n]
        return piece

    with jax.named_scope("proj_s"):
        total = jnp.zeros((128, 256), F32)
        for k, at in enumerate(chunks):
            loads[0, k].wait()
            loads[1, k].wait()
            turned = basis[at, :].T
            basis_t[:, at] = turned
            total += jnp.dot(turned, snap[at, :], preferred_element_type=F32)
        part_s[...] = total.T.reshape(16, 16, 128)
    with jax.named_scope("barrier_wait"):
        pl.semaphore_wait(barrier, 19)
    with jax.named_scope("send_s"):
        scatter(part_s, land_s, send_s, recv_s)
    for dx in (1, 2, 3):
        pl.semaphore_signal(here.at[0], inc=1, device_id=chip(dx, 0, 0), device_id_type=MESH)
    with jax.named_scope("proj_m"):
        total = jnp.zeros((128, 256), F32)
        for k, at in enumerate(chunks):
            loads[2, k].wait()
            total += jnp.dot(basis_t[:, at], rates[at, :], preferred_element_type=F32)
        part_m[...] = total.T.reshape(8, 2, 16, 128)
    with jax.named_scope("here0"):
        pl.semaphore_wait(here.at[0], 3)
        pl.semaphore_signal(here.at[1], inc=1, device_id=across, device_id_type=MESH)
    with jax.named_scope("send_m"):
        pltpu.make_async_remote_copy(
            src_ref=part_m.at[:, 1 - c], dst_ref=land_h, send_sem=send_h, recv_sem=recv_h,
            device_id=twin, device_id_type=MESH,
        ).start()

    height, width = row_out.shape[2], acc.shape[1]
    bases = ((0, rows * 524, height), (height, reg * 1048, width), (height + width, (rows + 1 - 2 * c) * 524, height))
    with jax.named_scope("picks"):
        for at, base, count in bases:
            pick_i[at:at + count, :], pick_j[at:at + count, :] = one_hot(base, count)

    def far(a, b, v):
        return turn(v, (1 - c) * a + c * b)

    pairs = [(a, b) for a in range(4) for b in range(4)]
    far_x, far_y, far_z = ({p: far(*p, v) for p in pairs} for v in (x, y, z))

    def target(dx, dy, dz):
        return device_at(far_x[dx, dy], far_y[dy, dz], far_z[dz, dx], c)

    def gather(buf, send, recv):
        flat = buf.reshape(buf.shape[0] * buf.shape[1], *buf.shape[2:])

        def scatter_out(first, last):
            for n, d in list(enumerate(chips))[first:last]:
                pltpu.make_async_remote_copy(
                    src_ref=buf.at[c, 0], dst_ref=buf.at[c, n], send_sem=send, recv_sem=recv.at[n // 16 if n > 6 else 8],
                    device_id=target(*d), device_id_type=MESH,
                ).start()

        def arrive_near():
            all_of(buf.at[c, pl.ds(0, 6)], send, recv.at[8]).wait_recv()

        def arrive(n):
            all_of(buf.at[c, pl.ds(0, 9 if n == 0 else 16)], send, recv.at[n]).wait_recv()

        def pass_on(n):
            at = pl.ds(n * 16, 16)
            pltpu.make_async_remote_copy(
                src_ref=buf.at[c, at], dst_ref=buf.at[c, at], send_sem=send, recv_sem=recv.at[4 + n],
                device_id=twin, device_id_type=MESH,
            ).start()

        def from_twin(n):
            all_of(buf.at[1 - c, pl.ds(n * 16, 16)], send, recv.at[4 + n]).wait_recv()

        def drain(count):
            all_of(flat.at[pl.ds(0, count)], send, recv.at[0]).wait_send()

        return scatter_out, arrive_near, arrive, pass_on, from_twin, drain

    s_out, s_near, s_arrive, s_pass, s_twin, s_drain = gather(states, sg_send, sg_recv)
    m_out, m_near, m_arrive, m_pass, m_twin, m_drain = gather(moments, mg_send, mg_recv)

    def features(core, n, parts):
        s = states[core, n * 16:(n + 1) * 16].reshape(256, 128)
        hi = s.astype(BF16)
        lo = (s - hi.astype(F32)).astype(BF16)
        split = jnp.concatenate([hi, lo], axis=1)

        def select(pick, at, count):
            e = pick[at:at + count, :]
            return lax.dot_general(
                jnp.concatenate([e, e], axis=1), split, (((1,), (1,)), ((), ())), preferred_element_type=F32
            )

        for at, base, count in parts[::-1]:
            k = lax.broadcasted_iota(jnp.int32, (128, 256), 0) + base
            plus = jnp.where(k < 128, 1.0, 0.0)
            a, b = select(pick_i, at, count), select(pick_j, at, count)
            feat[core, n, at:at + 128, :] = (a[:128] * (b[:128] + plus)).astype(BF16)
            feat[core, n, at + 128:at + count, :] = (a[128:] * b[128:]).astype(BF16)
        for src, dst in ((pl.ds(height + width, height), pl.ds(0, height)), (pl.ds(height, width),) * 2)[:len(parts) // 3 * 2]:
            pltpu.make_async_remote_copy(
                src_ref=feat.at[c, n, src], dst_ref=feat.at[c, n, dst], send_sem=f_send, recv_sem=f_recv.at[n],
                device_id=twin, device_id_type=MESH,
            ).start()

    times = 8 * 256
    out_rows, out_cols = gram.shape
    shared = pl.ds(0, height + width)

    def accumulate(n):
        if n < 3:
            all_of(feat.at[1 - c, n, shared], f_send, f_recv.at[n]).wait_recv()
        for q in range(2):
            pltpu.make_async_copy(feat.at[q, n, pl.ds(0, height)], row_out.at[q, n], out_sem.at[0]).start()
        lhs = jnp.concatenate([feat[q, n, :height, :] for q in range(2)], axis=1)
        for at in range(0, width, 256):
            to = min(at + 256, width)
            rhs = jnp.concatenate([feat[q, n, height + at:height + to, :] for q in range(2)], axis=1)
            part = lax.dot_general(lhs, rhs, (((1,), (1,)), ((), ())), preferred_element_type=F32)
            if n:
                part += acc[:, at:to]
            if n < 3:
                acc[:, at:to] = part
            else:
                to = min(to, out_cols)
                gram[:, at:to] = part[:out_rows, :to - at] * (1.0 / times)

    outs = [(moments, moments_out, 2), (gram, gram_out, 1)]

    with jax.named_scope("half_m"):
        all_of(land_h, send_h, recv_h).wait_recv()
        half_m[...] = part_m[:, c] + land_h[...]
        for n, (dy, dz, _) in enumerate(pair):
            to = ys[dy] * 2 + lax.rem(zl + dz, 2)
            pltpu.make_async_remote_copy(
                src_ref=half_m.at[to], dst_ref=land_m.at[n], send_sem=send_m, recv_sem=recv_m,
                device_id=(to * 2 + c, reg), device_id_type=MESH,
            ).start()
    with jax.named_scope("rs_s"):
        states[c, 0] = collect(part_s, rows, land_s, send_s, recv_s)
    with jax.named_scope("here1"):
        pl.semaphore_wait(here.at[1], 1)
    with jax.named_scope("s_out"):
        s_out(1, 32)

        @pl.when(c == 0)
        def _():
            s_out(32, 64)

    with jax.named_scope("near"):
        s_near()

    @pl.when(c == 1)
    def _():
        s_out(32, 48)


    for n in range(4):
        if n == 1:
            with jax.named_scope("m_out"):
                moments[c, 0] = collect(half_m, lax.div(rows, 2), land_m, send_m, recv_m).astype(BF16)
                m_out(1, 64)
        with jax.named_scope(f"a{n}"):
            s_arrive(n)
            if n == 0:
                pl.when(c == 1)(lambda: s_out(48, 64))
            if n == 3:
                s_pass(n)
        with jax.named_scope(f"f{n}"):
            features(c, n, bases if n < 3 else bases[:2])
        if n:
            with jax.named_scope(f"g{n - 1}"):
                accumulate(n - 1)
    with jax.named_scope("t3"):
        s_twin(3)
    with jax.named_scope("ft3"):
        features(1 - c, 3, bases[:2])
    with jax.named_scope("m_arrive"):
        m_near()
        for n in range(4):
            m_arrive(n)
            m_pass(n)
    with jax.named_scope("g3"):
        accumulate(3)
    pltpu.make_async_copy(gram, gram_out, out_sem.at[1]).start()
    with jax.named_scope("m_twin"):
        for k in range(4):
            m_twin(k)
    pltpu.make_async_copy(moments, moments_out, out_sem.at[2]).start()
    with jax.named_scope("drain"):
        all_of(land_s, send_s, recv_s).wait_send()
        all_of(land_m, send_m, recv_m).wait_send()
        all_of(land_h, send_h, recv_h).wait_send()
        s_drain(79)
        m_drain(127)
        all_of(feat.at[c, pl.ds(0, 3), shared], f_send, f_recv.at[0]).wait_send()
        for src, dst, n in [(row_out, row_out, 0)] + outs:
            pltpu.make_async_copy(src, dst, out_sem.at[n]).wait()


def finish_kernel(gram_ref, row_ref, moments_ref, gram_out, rhs_out, rhs_ref, sem):
    copy = pltpu.make_async_copy(gram_ref, gram_out, sem.at[0])
    copy.start()
    blocks = [(q, n) for q in range(2) for n in range(4)]
    with jax.named_scope("rhs"):
        rhs = jnp.dot(
            jnp.concatenate([row_ref[q, n] for q, n in blocks], axis=1),
            jnp.concatenate([moments_ref[q, n * 16:(n + 1) * 16].reshape(256, 128) for q, n in blocks], axis=0),
            preferred_element_type=F32,
        )
        rhs_ref[...] = rhs[:rhs_ref.shape[0]] * (1.0 / (256 * len(blocks)))
    with jax.named_scope("k2wait"):
        rhs_copy = pltpu.make_async_copy(rhs_ref, rhs_out, sem.at[1])
        rhs_copy.start()
        copy.wait()
        rhs_copy.wait()


def per_device(snapshots, rates, basis):
    n, t = snapshots.shape
    rank = basis.shape[1]
    width = rank + rank * (rank + 1) // 2
    assert rank == 128 and t == 256 and n == sum(CHUNKS)
    assert lax.axis_size("rows") == 16 and lax.axis_size("reg") == 8
    row_width, col_width = width // 16, width // 8
    row_pad, col_pad = pl.cdiv(row_width, 16) * 16, pl.cdiv(col_width, 16) * 16
    dma = pltpu.SemaphoreType.DMA
    gram, row_feat, moments = pl.pallas_call(
        exchange_kernel,
        out_shape=(
            jax.ShapeDtypeStruct((row_width, col_width), F32),
            jax.ShapeDtypeStruct((2, 4, row_pad, t), BF16),
            jax.ShapeDtypeStruct((2, 64, 16, rank), BF16),
        ),
        in_specs=[pl.BlockSpec(memory_space=pl.ANY)] * 3,
        out_specs=[pl.BlockSpec(memory_space=pl.ANY)] * 3,
        scratch_shapes=[
            pltpu.VMEM((2, 64, 16, rank), F32),
            pltpu.VMEM((2, 64, 16, rank), BF16),
            pltpu.VMEM((2, 4, 2 * row_pad + col_pad, t), BF16),
            pltpu.VMEM((row_pad, col_pad), F32),
            pltpu.VMEM((row_width, col_width), F32),
            pltpu.VMEM((n, t), BF16),
            pltpu.VMEM((n, t), BF16),
            pltpu.VMEM((n, rank), BF16),
            pltpu.VMEM((rank, n), BF16),
            pltpu.VMEM((16, 16, rank), F32),
            pltpu.VMEM((8, 2, 16, rank), F32),
            pltpu.VMEM((8, 16, rank), F32),
            pltpu.VMEM((15, 16, rank), F32),
            pltpu.VMEM((7, 16, rank), F32),
            pltpu.VMEM((8, 16, rank), F32),
            pltpu.VMEM((2 * row_pad + col_pad, rank), BF16),
            pltpu.VMEM((2 * row_pad + col_pad, rank), BF16),
            dma((3, len(CHUNKS))),
            dma, dma, dma, dma, dma, dma,
            dma, dma((9,)), dma, dma((9,)), dma, dma((3,)), dma((3,)), pltpu.SemaphoreType.REGULAR((2,)),
        ],
        compiler_params=pltpu.CompilerParams(
            collective_id=0, has_side_effects=True, vmem_limit_bytes=VMEM_KIB << 10
        ),
        name="exchange",
    )(*[pltpu.with_memory_space_constraint(a, pltpu.MemorySpace.HBM) for a in (snapshots, rates, basis)])
    return pl.pallas_call(
        finish_kernel,
        out_shape=(
            jax.ShapeDtypeStruct((row_width, col_width), F32),
            jax.ShapeDtypeStruct((row_width, rank), F32),
        ),
        in_specs=[
            pl.BlockSpec(memory_space=pl.ANY),
            pl.BlockSpec(memory_space=pltpu.VMEM),
            pl.BlockSpec(memory_space=pltpu.VMEM),
        ],
        out_specs=[pl.BlockSpec(memory_space=pl.ANY)] * 2,
        scratch_shapes=[pltpu.VMEM((row_width, rank), F32), dma((2,))],
        compiler_params=pltpu.CompilerParams(vmem_limit_bytes=16 << 20),
        name="finish",
    )(gram, row_feat, moments)


def solution(mesh):
    return jax.shard_map(
        per_device,
        mesh=mesh,
        in_specs=(P("rows", "reg"), P("rows", "reg"), P("rows", None)),
        out_specs=(P("rows", "reg"), P("rows", None)),
        check_vma=False,
    )
```
